32 devices in a mesh: dp: 4 (over x, core), ulysses: 2 (over y), expert: 4 (over z).
Axes of the slice: x: 2, y: 2, z: 4, core: 2. Of those that a mesh axis runs over, the one named last changes fastest.
Arguments:
- residual: bfloat16 [4096, 4096], P(('dp', 'ulysses', 'expert')), may hold values from -6 to 6
- norm_gain: float32 [4096], replicated, may hold values from 0.1 to 1.9
- grad_out: bfloat16 [4096, 4096], P(('dp', 'ulysses', 'expert')), may hold values from -6 to 6
- expert_ids: int32 [4096, 2], P(('dp', 'ulysses', 'expert')), may hold values from 0 to 3, all different within a row; in each aligned block of 128 rows (0 to 127, 128 to 255, ...) at most 96 rows name the same one
- route_weights: bfloat16 [4096, 2], P(('dp', 'ulysses', 'expert')), may hold values from 0.099609375 to 1
- weight_in: bfloat16 [4, 4096, 1536], P('expert'), may hold values from -0.09375 to 0.09375
- weight_down: bfloat16 [4, 768, 4096], P('expert'), may hold values from -0.21875 to 0.21875
Outputs:
- grad_residual: bfloat16 [4096, 4096], P(('dp', 'ulysses', 'expert'))
- route_grad: bfloat16 [4096, 2], P(('dp', 'ulysses', 'expert'))
- grad_in: float32 [4, 4096, 1536], P('expert', ('dp', 'ulysses'))
- grad_down: float32 [4, 4096, 768], P('expert', ('dp', 'ulysses'))
The draws below stay inside these ranges and needn't reach their ends.
Inputs may be any that keep to these rules, and one draw needn't show every extreme that they name: `expert_ids`: each row names 2 different experts. Among the rows of one device no expert is named more than 96 times, and in some devices' rows one expert is named exactly 96 times.
All inputs are finite; a program needn't handle non-finite values.
Results may differ from the reference program's by a relative error of at most 0.017.
Values may be sent and summed in bfloat16 or wider, within the bound.
A program may use at most 192 MiB of HBM per device.

```python
import math
import jax
import jax.numpy as jnp
import numpy as np
from jax import lax

D = 4096
HID = 768
TOPK = 2
TOK_DEV = 128
EXPERTS = 4
TOKENS = 4096
CAP = 96
N_DP = 4
N_ULYSSES = 2
N_EXPERT = 4
DEVICES = 32


def raised(array, rng, source, target, shards_of, factor):
    def block_of(axis_at):
        return (jnp.arange(array.shape[axis_at]) // (array.shape[axis_at] // shards_of)).reshape((-1,) + (1,) * (array.ndim - 1 - axis_at))

    one_side = jax.random.permutation(rng, shards_of)[block_of(target)]
    far = (block_of(target) + shards_of // 2) % shards_of
    return jnp.where((block_of(source) == one_side) | (block_of(source) == far), factor * array, array)


def shard_levels(stream_key, extent, cuts, least, top_value):
    gain = 1.0
    for dim, parts in cuts:
        draws = jax.random.uniform(jax.random.fold_in(jax.random.fold_in(stream_key, 6), dim), (parts,), jnp.float32, least / len(cuts), top_value / len(cuts))
        gain = gain * jnp.repeat(jnp.exp(draws), extent[dim] // parts).reshape((-1,) + (1,) * (len(extent) - 1 - dim))
    return gain


def shared_out(stream_key, own, number, rows, count, top, limit, skew):
    ranking = jax.random.permutation(stream_key, count)
    crowded, ordinary = portions_of(count, rows * top, limit, skew, True), portions_of(count, rows * top, limit, skew, False)
    places = jnp.arange(count)

    def named(lengths, turn):
        used = int((lengths > 0).sum())
        fixed = max(1, used // 4)
        moved = fixed + (places - fixed + turn * (used - fixed)) % max(1, count - fixed)
        return jnp.zeros((count,), jnp.int32).at[ranking[jnp.where(places < fixed, places, moved)]].set(jnp.asarray(lengths, jnp.int32))

    lengths = jnp.where(number % 4 == 0, named(crowded, number // 4), named(ordinary, number - number // 4 - 1))
    mixed = jax.random.permutation(jax.random.fold_in(own, 3), count)
    source_of, receiver = mixed[0:count // 2 * 2:2], mixed[1:count // 2 * 2:2]
    room = jnp.minimum(lengths[source_of] - 1, limit - lengths[receiver]) // 2
    room = jnp.where((source_of == ranking[0]) | (receiver == ranking[0]) | (lengths[receiver] == 0), 0, jnp.maximum(room, 0))
    moved = jax.random.randint(jax.random.fold_in(own, 4), (count // 2,), 0, 1 << 20) % (room + 1)
    lengths = lengths.at[source_of].add(-moved).at[receiver].add(moved)
    labels = jnp.searchsorted(jnp.cumsum(lengths), jnp.arange(rows * top), side="right").astype(jnp.int32)
    listing = labels.reshape(top, rows).T
    listing = listing[jax.random.permutation(jax.random.fold_in(own, 1), rows)]
    turn = jax.random.randint(jax.random.fold_in(own, 2), (rows, 1), 0, top)
    return jnp.take_along_axis(listing, (jnp.arange(top)[None, :] + turn) % top, axis=1)


def portions_of(amount, total, most, skew, full):
    portions = [(1 << 20) // math.isqrt(standing ** skew) + 1 for standing in range(1, amount + 1)]
    largest = most if full else min(most, max(-(-total // amount), total * portions[0] // sum(portions)))
    least = 1 if total - largest >= amount - 1 else 0
    holding, rest = [largest] + [least] * (amount - 1), total - largest - least * (amount - 1)
    while rest > 0:
        candidates = [i for i in range(1, amount) if holding[i] < largest] or [i for i in range(1, amount) if holding[i] < most]
        pool, remaining = sum([portions[i] for i in candidates]), rest
        for i in candidates:
            more = min(most - holding[i], max(1, remaining * portions[i] // pool), rest)
            holding[i] = holding[i] + more
            rest = rest - more
    return np.array(holding)


def gaussian(stream_key, extent, spread, most, split=(), kind=jnp.bfloat16):
    entries = jax.random.normal(stream_key, extent, jnp.float32) * spread
    if len(split) > 0:
        entries = shard_levels(stream_key, extent, split, -0.22, 0.18) * entries
    return jnp.clip(entries, min=-most, max=most).astype(kind)


def heavy_noise(own_key, shape, width, limit, split, heavy, kind=jnp.bfloat16):
    array = width * jax.random.normal(own_key, shape, jnp.float32)
    if split:
        array = array * shard_levels(own_key, shape, split, -0.22, 0.18)
    return jnp.clip(raised(array, jax.random.fold_in(own_key, 3), *heavy), -limit, limit).astype(kind)


def setup_inputs(seed: int = 0) -> dict:
    seeds = jax.random.split(jax.random.key(seed), 8)
    residual = heavy_noise(seeds[0], (TOKENS, D), 1.0, 6.0, ((0, 32),), (0, 1, 32, 2.75))
    norm_gain = jnp.clip(1.0 + 0.18 * jax.random.normal(seeds[1], (D,), jnp.float32), 0.1, 1.9)
    grad_out = heavy_noise(seeds[2], (TOKENS, D), 1.0, 6.0, ((0, 32),), (0, 1, 32, 2.75))
    expert_ids_keys = jax.random.split(jax.random.fold_in(seeds[3], 1), TOKENS // TOK_DEV)
    expert_ids_turns = jax.random.permutation(jax.random.fold_in(seeds[3], 3), TOKENS // TOK_DEV)
    expert_ids = jax.vmap(lambda own, number: shared_out(jax.random.fold_in(seeds[3], 2), own, number, TOK_DEV, EXPERTS, TOPK, CAP, 2))(expert_ids_keys, expert_ids_turns).reshape((TOKENS, TOPK))
    route_weights = jnp.clip(0.099609375 + 0.9003906 * jax.random.uniform(seeds[4], (TOKENS, TOPK), jnp.float32) ** shard_levels(seeds[4], (TOKENS, TOPK), ((0, 32),), -0.2, 0.2), 0.099609375, 1.0).astype(jnp.bfloat16)
    weight_in = gaussian(seeds[5], (EXPERTS, D, 2 * HID), D ** -0.5, 0.09375, ((0, 4),))
    weight_down = gaussian(seeds[6], (EXPERTS, HID, D), HID ** -0.5, 0.21875, ((0, 4),))
    return dict(residual=residual, norm_gain=norm_gain, grad_out=grad_out, expert_ids=expert_ids, route_weights=route_weights, weight_in=weight_in, weight_down=weight_down)


eps = 1e-06

def slot_positions(expert_ids):
    flat_ids = expert_ids.reshape(DEVICES, TOK_DEV * TOPK).astype(jnp.int32)
    one_hot = (flat_ids[:, :, None] == jnp.arange(EXPERTS, dtype=jnp.int32)[None, None, :]).astype(jnp.int32)
    ranks = jnp.cumsum(one_hot, axis=1) - one_hot
    slots = lax.optimization_barrier(jnp.sum(ranks * one_hot, axis=2)).astype(jnp.int32)
    blocks = (jnp.arange(DEVICES, dtype=jnp.int32) % N_EXPERT)[:, None]
    return (flat_ids * (N_EXPERT * CAP) + blocks * CAP + slots).astype(jnp.int32)

def reference(residual, norm_gain, grad_out, expert_ids, route_weights, weight_in, weight_down):
    groups = N_DP * N_ULYSSES
    members = N_EXPERT * TOK_DEV
    slots_all = EXPERTS * N_EXPERT * CAP
    resid = residual.astype(jnp.float32)
    inv_rms = lax.rsqrt(lax.optimization_barrier(jnp.mean(resid * resid, axis=-1, keepdims=True)) + eps)
    unit_rows = resid * inv_rms
    normed = (unit_rows * norm_gain).astype(jnp.bfloat16)
    positions = slot_positions(expert_ids).reshape(groups, members * TOPK)
    token_local = (jnp.arange(members * TOPK, dtype=jnp.int32) // TOPK).astype(jnp.int32)
    weights_grouped = route_weights.reshape(groups, members * TOPK)
    normed_grouped = normed.reshape(groups, members, D)
    grad_grouped = grad_out.reshape(groups, members, D)
    win = weight_in.astype(jnp.float32)
    wdown = weight_down.astype(jnp.float32)

    def group_step(carry, inputs):
        acc_in, acc_down = carry
        where, weights, normed_rows, grad_rows = inputs
        source = jnp.full((slots_all,), members, jnp.int32).at[where].set(token_local)
        slot_weight = jnp.zeros((slots_all,), jnp.bfloat16).at[where].set(weights)
        padded_normed = jnp.concatenate([normed_rows, jnp.zeros((1, D), jnp.bfloat16)], 0)
        padded_grad = jnp.concatenate([grad_rows, jnp.zeros((1, D), jnp.bfloat16)], 0)
        sent_normed = padded_normed[source].reshape(EXPERTS, N_EXPERT * CAP, D).astype(jnp.float32)
        sent_grad = padded_grad[source].reshape(EXPERTS, N_EXPERT * CAP, D).astype(jnp.float32)
        slot_col = slot_weight.reshape(EXPERTS, N_EXPERT * CAP, 1).astype(jnp.float32)
        proj = jnp.einsum('erd,edh->erh', sent_normed, win)
        gate_proj = proj[..., :HID]
        up_proj = proj[..., HID:]
        sigmoid_gate = jax.nn.sigmoid(gate_proj)
        silu_gate = gate_proj * sigmoid_gate
        hidden = lax.optimization_barrier((silu_gate * up_proj).astype(jnp.bfloat16)).astype(jnp.float32)
        back_proj = jnp.einsum('erd,ehd->erh', sent_grad, wdown)
        slot_grad = lax.optimization_barrier(jnp.sum(back_proj * hidden, axis=-1)).astype(jnp.bfloat16)
        grad_hidden = slot_col * back_proj
        d_gate = grad_hidden * up_proj * sigmoid_gate * (1.0 + gate_proj * (1.0 - sigmoid_gate))
        d_up = grad_hidden * silu_gate
        d_proj = lax.optimization_barrier(jnp.concatenate([d_gate, d_up], -1).astype(jnp.bfloat16)).astype(jnp.float32)
        slot_normed = jnp.einsum('erh,edh->erd', d_proj, win).astype(jnp.bfloat16)
        scaled = lax.optimization_barrier((slot_col * sent_grad).astype(jnp.bfloat16)).astype(jnp.float32)
        part_in = lax.optimization_barrier(jnp.einsum('erd,erh->edh', sent_normed, d_proj).astype(jnp.bfloat16)).astype(jnp.float32)
        part_down = lax.optimization_barrier(jnp.einsum('erd,erh->edh', scaled, hidden).astype(jnp.bfloat16)).astype(jnp.float32)
        flat_normed = slot_normed.reshape(slots_all, D).astype(jnp.float32)
        token_normed = lax.optimization_barrier(jnp.sum(flat_normed[where].reshape(members, TOPK, D), axis=1))
        token_route = slot_grad.reshape(slots_all)[where].reshape(members, TOPK)
        return ((acc_in + part_in, acc_down + part_down), (token_normed, token_route))
    init = (jnp.zeros((EXPERTS, D, 2 * HID), jnp.float32), jnp.zeros((EXPERTS, D, HID), jnp.float32))
    (grad_in, grad_down), (grad_normed, route_grad) = lax.scan(group_step, init, (positions, weights_grouped, normed_grouped, grad_grouped))
    grad_normed = grad_normed.reshape(TOKENS, D)
    scaled_normed = grad_normed * norm_gain
    branch = inv_rms * (scaled_normed - unit_rows * lax.optimization_barrier(jnp.mean(scaled_normed * unit_rows, axis=-1, keepdims=True)))
    grad_residual = (grad_out.astype(jnp.float32) + branch).astype(jnp.bfloat16)
    return (grad_residual, route_grad.reshape(TOKENS, TOPK), grad_in, grad_down)
```

```python
import jax
import jax.numpy as jnp
from jax import lax
from jax.sharding import PartitionSpec as P

eps = 1e-06
f32 = jnp.float32
bf16 = jnp.bfloat16


def dot(left, right):
    return jnp.dot(left, right, preferred_element_type=f32)


def contract_rows(left, right):
    return lax.dot_general(left, right, (((0,), (0,)), ((), ())), preferred_element_type=f32)


def contract_cols(left, right):
    return lax.dot_general(left, right, (((1,), (1,)), ((), ())), preferred_element_type=f32)


def selection(ids, expert, capacity):
    tokens = ids.shape[0]
    hit = jnp.any(ids == expert, axis=1)
    row = lax.broadcasted_iota(jnp.int32, (tokens, tokens), 0)
    col = lax.broadcasted_iota(jnp.int32, (tokens, tokens), 1)
    rank = jnp.sum(jnp.where((row < col) & hit[:, None], 1, 0), axis=0)
    slots = lax.broadcasted_iota(jnp.int32, (capacity, tokens), 0)
    return ((slots == rank[None, :]) & hit[None, :]).astype(bf16)


def line_forward(rows, mine, to_last, to_first, n):
    raw = [None] * n
    packed = [[] for _ in range(n)]
    raw_parts = [[] for _ in range(n)]
    right, left = rows, rows
    for t in range(1, n):
        packed[t].append(
            lax.ppermute(dot(to_last[t - 1], right).astype(bf16), "expert", [(n - 2, n - 1)])
        )
        packed[n - t].append(
            lax.ppermute(dot(to_first[(n - t + 1) % n], left).astype(bf16), "expert", [(1, 0)])
        )
        pairs_right = [(j, j + 1) for j in range(t - 1, n - 2)]
        if pairs_right:
            right = lax.ppermute(right, "expert", pairs_right)
            left = lax.ppermute(left, "expert", [(n - 1 - a, n - 1 - b) for a, b in pairs_right])
            raw_parts[t].append(right)
            raw_parts[n - t].append(left)
    blocks = [dot(mine[0], rows).astype(bf16)]
    for k in range(1, n):
        block = None
        if raw_parts[k]:
            block = dot(mine[k], sum(raw_parts[k][1:], raw_parts[k][0])).astype(bf16)
        for part in packed[k]:
            block = part if block is None else block + part
        blocks.append(block)
    return blocks


def line_backward(blocks, mine, to_last, to_first, n):
    back_left, back_right = None, None
    for t in range(n - 1, 0, -1):
        new = []
        for k, got, ends, first in (
            (t, back_left, to_last, True),
            (n - t, back_right, to_first, False),
        ):
            flip = (lambda j: j) if first else (lambda j: n - 1 - j)
            packed = lax.ppermute(blocks[k], "expert", [(flip(n - 1), flip(n - 2))])
            came = (k - 1) % n if first else (k + 1) % n
            total = contract_rows(ends[came], packed)
            pairs = [(flip(j + 1), flip(j)) for j in range(t - 1, n - 2)]
            if pairs:
                held = contract_rows(mine[k], blocks[k])
                if got is not None:
                    held = held + got
                total = total + lax.ppermute(held.astype(bf16), "expert", pairs).astype(f32)
            new.append(total)
        back_left, back_right = new
    return contract_rows(mine[0], blocks[0]) + back_left + back_right


def per_device(residual, norm_gain, grad_out, expert_ids, route_weights, weight_in, weight_down):
    tok_rows, width = residual.shape
    topk = expert_ids.shape[1]
    hid = weight_down.shape[1]
    n = lax.axis_size("expert")
    n_dp, n_ul = lax.axis_size("dp"), lax.axis_size("ulysses")
    groups = n_dp * n_ul
    me = lax.axis_index("expert")
    capacity = min(tok_rows, 3 * tok_rows * topk // (2 * n))
    w_in, w_down = weight_in[0], weight_down[0]

    routes = jnp.concatenate([expert_ids.astype(f32), route_weights.astype(f32)], axis=1).T
    routes_of = [routes] + [
        lax.ppermute(routes, "expert", [(j, (j + k) % n) for j in range(n)]) for k in range(1, n)
    ]
    ids_of = [r[:topk].T.astype(jnp.int32) for r in routes_of]
    mine = [selection(ids, me, capacity) for ids in ids_of]
    to_last = [selection(ids, n - 1, capacity) for ids in ids_of]
    to_first = [selection(ids, 0, capacity) for ids in ids_of]
    weight_of = []
    for r, ids, m in zip(routes_of, ids_of, mine):
        w_tok = jnp.sum(jnp.where(ids == me, r[topk:].T, 0.0), axis=1, keepdims=True)
        weight_of.append(dot(m, w_tok.astype(bf16)))
    weight_col = jnp.concatenate(weight_of, axis=0)

    resid = residual.astype(f32)
    inv_rms = lax.rsqrt(jnp.mean(resid * resid, axis=-1, keepdims=True) + eps)
    unit_rows = resid * inv_rms
    normed = (unit_rows * norm_gain).astype(bf16)

    normed_rows = jnp.concatenate(line_forward(normed, mine, to_last, to_first, n), axis=0)
    grad_rows = jnp.concatenate(line_forward(grad_out, mine, to_last, to_first, n), axis=0)

    spot = lax.axis_index("dp") * n_ul + lax.axis_index("ulysses")
    part = width // groups

    def to_peers(rows):
        out = []
        for mask in range(groups):
            piece = lax.dynamic_slice_in_dim(rows, (spot ^ mask) * part, part, axis=1)
            if mask:
                piece = lax.ppermute(
                    piece, ("dp", "ulysses"), [(j, j ^ mask) for j in range(groups)]
                )
            out.append(piece)
        return out

    cols_normed = to_peers(normed_rows)

    proj = dot(normed_rows, w_in)
    gate, up = proj[:, :hid], proj[:, hid:]
    sigmoid_gate = jax.nn.sigmoid(gate)
    silu_gate = gate * sigmoid_gate
    hidden = (silu_gate * up).astype(bf16)
    scaled = (weight_col * grad_rows.astype(f32)).astype(bf16)
    cols_scaled = to_peers(scaled)
    back = contract_cols(grad_rows, w_down)
    slot_grad = jnp.sum(back * hidden.astype(f32), axis=1).astype(bf16)
    grad_hidden = weight_col * back
    d_gate = grad_hidden * up * sigmoid_gate * (1.0 + gate * (1.0 - sigmoid_gate))
    d_up = grad_hidden * silu_gate
    d_proj = jnp.concatenate([d_gate, d_up], axis=1).astype(bf16)
    inner = jnp.concatenate([d_proj, hidden], axis=1)

    def swap(rows, mask):
        return lax.ppermute(rows, ("dp", "ulysses"), [(j, j ^ mask) for j in range(groups)])

    inner_of = [None] * groups
    inner_of[0] = inner
    if groups == 8 and n_ul == 2:
        across_y, across_core, across_x = 1, 2, 4
        half = inner.shape[0] // 2
        top, low = inner[:half], inner[half:]
        top_x, low_y = swap(top, across_x), swap(low, across_y)
        low_x, top_y = swap(low, across_x), swap(top, across_y)
        top_xy, low_xy = swap(top_x, across_y), swap(low_y, across_x)
        inner_of[across_x] = jnp.concatenate([top_x, low_x], axis=0)
        inner_of[across_y] = jnp.concatenate([top_y, low_y], axis=0)
        inner_of[across_x | across_y] = jnp.concatenate([top_xy, low_xy], axis=0)
        inner_of[across_core] = swap(inner, across_core)
        for top_part, low_part, mask in (
            (top_x, low_x, across_x),
            (top_y, low_y, across_y),
            (top_xy, low_xy, across_x | across_y),
        ):
            inner_of[mask | across_core] = jnp.concatenate(
                [swap(top_part, across_core), swap(low_part, across_core)], axis=0
            )
    else:
        for mask in range(1, groups):
            inner_of[mask] = swap(inner, mask)

    slot_normed = contract_cols(d_proj, w_in).astype(bf16)
    slot_blocks = [slot_normed[k * capacity : (k + 1) * capacity] for k in range(n)]
    grad_normed = line_backward(slot_blocks, mine, to_last, to_first, n)

    token_route = jnp.zeros((tok_rows, topk), f32)
    for k in range(n):
        values = slot_grad[k * capacity : (k + 1) * capacity].reshape(1, capacity)
        if k:
            values = lax.ppermute(values, "expert", [(j, (j - k) % n) for j in range(n)])
        expert = (me + k) % n
        got = contract_rows(selection(expert_ids, expert, capacity), values.reshape(capacity, 1))
        token_route = token_route + jnp.where(expert_ids == expert, got, 0.0)
    route_grad = token_route.astype(bf16)

    scaled_normed = grad_normed * norm_gain
    branch = inv_rms * (
        scaled_normed - unit_rows * jnp.mean(scaled_normed * unit_rows, axis=-1, keepdims=True)
    )
    grad_residual = (grad_out.astype(f32) + branch).astype(bf16)

    grad_in = jnp.zeros((), f32)
    grad_down = jnp.zeros((), f32)
    if groups == 8 and n_ul == 2:
        bundles = [[0, 2], [4, 6, 1, 3], [5, 7]]
    else:
        bundles = [[mask] for mask in range(groups)]
    for bundle in bundles:
        inners = jnp.concatenate([inner_of[m] for m in bundle], axis=0)
        left_in = jnp.concatenate([cols_normed[m] for m in bundle], axis=0)
        left_down = jnp.concatenate([cols_scaled[m] for m in bundle], axis=0)
        grad_in = grad_in + contract_rows(left_in, inners[:, : 2 * hid])
        grad_down = grad_down + contract_rows(left_down, inners[:, 2 * hid :])
    return (grad_residual, route_grad, grad_in[None], grad_down[None])


def solution(mesh):
    rows = P(("dp", "ulysses", "expert"), None)
    return jax.shard_map(
        per_device,
        mesh=mesh,
        in_specs=(rows, P(), rows, rows, rows, P("expert", None, None), P("expert", None, None)),
        out_specs=(
            rows,
            rows,
            P("expert", ("dp", "ulysses"), None),
            P("expert", ("dp", "ulysses"), None),
        ),
        check_vma=False,
    )
```

```python
import jax
import jax.numpy as jnp
from jax import lax
from jax.sharding import PartitionSpec as P

eps = 1e-06
f32 = jnp.float32
bf16 = jnp.bfloat16


def dot(left, right):
    return jnp.dot(left, right, preferred_element_type=f32)


def contract_rows(left, right):
    return lax.dot_general(left, right, (((0,), (0,)), ((), ())), preferred_element_type=f32)


def contract_cols(left, right):
    return lax.dot_general(left, right, (((1,), (1,)), ((), ())), preferred_element_type=f32)


def after(value, *others):
    return lax.optimization_barrier((value, *others))[0]


def selection(ids, expert, capacity):
    tokens = ids.shape[0]
    hit = jnp.any(ids == expert, axis=1)
    row = lax.broadcasted_iota(jnp.int32, (tokens, tokens), 0)
    col = lax.broadcasted_iota(jnp.int32, (tokens, tokens), 1)
    rank = jnp.sum(jnp.where((row < col) & hit[:, None], 1, 0), axis=0)
    slots = lax.broadcasted_iota(jnp.int32, (capacity, tokens), 0)
    return ((slots == rank[None, :]) & hit[None, :]).astype(bf16)


def line_forward(rows, mine, to_last, to_first, n):
    raw = [None] * n
    packed = [[] for _ in range(n)]
    raw_parts = [[] for _ in range(n)]
    right, left = rows, rows
    for t in range(1, n):
        ends = (
            dot(to_last[t - 1], right).astype(bf16),
            dot(to_first[(n - t + 1) % n], left).astype(bf16),
        )
        packed[t].append(lax.ppermute(ends[0], "expert", [(n - 2, n - 1)]))
        packed[n - t].append(lax.ppermute(ends[1], "expert", [(1, 0)]))
        pairs_right = [(j, j + 1) for j in range(t - 1, n - 2)]
        if pairs_right:
            right = lax.ppermute(right, "expert", pairs_right)
            left = lax.ppermute(left, "expert", [(n - 1 - a, n - 1 - b) for a, b in pairs_right])
            raw_parts[t].append(right)
            raw_parts[n - t].append(left)
    blocks = [dot(mine[0], rows).astype(bf16)]
    for k in range(1, n):
        block = None
        if raw_parts[k]:
            block = dot(mine[k], sum(raw_parts[k][1:], raw_parts[k][0])).astype(bf16)
        for part in packed[k]:
            block = part if block is None else block + part
        blocks.append(block)
    return blocks, (raw_parts[1][:1] + raw_parts[n - 1][:1]), ends


def line_backward(blocks, mine, to_last, to_first, n):
    back_left, back_right = None, None
    for t in range(n - 1, 0, -1):
        new = []
        for k, got, ends, first in (
            (t, back_left, to_last, True),
            (n - t, back_right, to_first, False),
        ):
            flip = (lambda j: j) if first else (lambda j: n - 1 - j)
            packed = lax.ppermute(blocks[k], "expert", [(flip(n - 1), flip(n - 2))])
            came = (k - 1) % n if first else (k + 1) % n
            total = contract_rows(ends[came], packed)
            pairs = [(flip(j + 1), flip(j)) for j in range(t - 1, n - 2)]
            if pairs:
                held = contract_rows(mine[k], blocks[k])
                if got is not None:
                    held = held + got
                total = total + lax.ppermute(held.astype(bf16), "expert", pairs).astype(f32)
            new.append(total)
        back_left, back_right = new
    return contract_rows(mine[0], blocks[0]) + back_left + back_right


def per_device(residual, norm_gain, grad_out, expert_ids, route_weights, weight_in, weight_down):
    tok_rows, width = residual.shape
    topk = expert_ids.shape[1]
    hid = weight_down.shape[1]
    n = lax.axis_size("expert")
    n_dp, n_ul = lax.axis_size("dp"), lax.axis_size("ulysses")
    groups = n_dp * n_ul
    me = lax.axis_index("expert")
    capacity = min(tok_rows, 3 * tok_rows * topk // (2 * n))
    w_in, w_down = weight_in[0], weight_down[0]

    routes = jnp.concatenate([expert_ids.astype(f32), route_weights.astype(f32)], axis=1).T
    routes_of = [routes] + [
        lax.ppermute(routes, "expert", [(j, (j + k) % n) for j in range(n)]) for k in range(1, n)
    ]
    ids_of = [r[:topk].T.astype(jnp.int32) for r in routes_of]
    mine = [selection(ids, me, capacity) for ids in ids_of]
    to_last = [selection(ids, n - 1, capacity) for ids in ids_of]
    to_first = [selection(ids, 0, capacity) for ids in ids_of]
    weight_of = []
    for r, ids, m in zip(routes_of, ids_of, mine):
        w_tok = jnp.sum(jnp.where(ids == me, r[topk:].T, 0.0), axis=1, keepdims=True)
        weight_of.append(dot(m, w_tok.astype(bf16)))

    resid = residual.astype(f32)
    inv_rms = lax.rsqrt(jnp.mean(resid * resid, axis=-1, keepdims=True) + eps)
    unit_rows = resid * inv_rms
    normed = (unit_rows * norm_gain).astype(bf16)

    order = [0, n // 2] + [k for k in range(1, n) if k != n // 2]
    place = {k: i for i, k in enumerate(order)}
    normed_blocks, first_hops, _ = line_forward(normed, mine, to_last, to_first, n)
    grad_blocks, _, last_sent = line_forward(after(grad_out, *first_hops), mine, to_last, to_first, n)
    normed_rows = jnp.concatenate([normed_blocks[k] for k in order], axis=0)
    weight_col = jnp.concatenate([weight_of[k] for k in order], axis=0)
    grad_rows = jnp.concatenate([grad_blocks[k] for k in order], axis=0)

    spot = lax.axis_index("dp") * n_ul + lax.axis_index("ulysses")
    part = width // groups

    def to_peers(rows):
        pieces = rows.reshape(rows.shape[0], groups, part).transpose(1, 0, 2)
        return lax.all_to_all(pieces, ("dp", "ulysses"), split_axis=0, concat_axis=0, tiled=True)

    cols_normed = to_peers(normed_rows)

    proj = dot(normed_rows, w_in)
    gate, up = proj[:, :hid], proj[:, hid:]
    sigmoid_gate = jax.nn.sigmoid(gate)
    silu_gate = gate * sigmoid_gate
    hidden = (silu_gate * up).astype(bf16)
    early = 2 * capacity
    scaled_early = jnp.concatenate(
        [(weight_of[k] * grad_blocks[k].astype(f32)).astype(bf16) for k in order[:2]], axis=0
    )
    cols_early = to_peers(after(scaled_early, cols_normed, *last_sent))
    grad_rows = after(grad_rows, cols_normed, proj)
    scaled_late = (weight_col[early:] * grad_rows[early:].astype(f32)).astype(bf16)
    cols_late = to_peers(after(scaled_late, cols_early))
    back = contract_cols(grad_rows, w_down)
    slot_grad = jnp.sum(back * hidden.astype(f32), axis=1).astype(bf16)
    grad_hidden = weight_col * back
    d_gate = grad_hidden * up * sigmoid_gate * (1.0 + gate * (1.0 - sigmoid_gate))
    d_up = grad_hidden * silu_gate
    d_proj = jnp.concatenate([d_gate, d_up], axis=1).astype(bf16)
    inner = lax.optimization_barrier(jnp.concatenate([d_proj, hidden], axis=1))
    d_proj = inner[:, : 2 * hid]

    def swap(rows, mask):
        return lax.ppermute(rows, ("dp", "ulysses"), [(j, j ^ mask) for j in range(groups)])

    inner_of = [None] * groups
    inner_of[0] = inner
    if groups == 8 and n_ul == 2:
        across_y, across_core, across_x = 1, 2, 4
        half = inner.shape[0] // 2
        top, low = inner[:half], inner[half:]
        top_x, low_y = swap(top, across_x), swap(low, across_y)
        low_x, top_y = swap(low, across_x), swap(top, across_y)
        top_xy, low_xy = swap(top_x, across_y), swap(low_y, across_x)
        inner_of[across_x] = jnp.concatenate([top_x, low_x], axis=0)
        inner_of[across_y] = jnp.concatenate([top_y, low_y], axis=0)
        inner_of[across_x | across_y] = jnp.concatenate([top_xy, low_xy], axis=0)
        own_other = swap(inner, across_core)
        near = swap(jnp.concatenate([top_x, low_y], axis=0), across_core)
        later = swap(jnp.concatenate([low_x, top_y], axis=0), across_core)
        far = swap(inner_of[across_x | across_y], across_core)
        inner_of[across_core] = own_other
        inner_of[across_x | across_core] = jnp.concatenate([near[:half], later[:half]], axis=0)
        inner_of[across_y | across_core] = jnp.concatenate([later[half:], near[half:]], axis=0)
        inner_of[across_x | across_y | across_core] = far
    else:
        for mask in range(1, groups):
            inner_of[mask] = swap(inner, mask)

    slot_normed = contract_cols(d_proj, w_in).astype(bf16)
    token_route = jnp.zeros((tok_rows, topk), f32)
    for k in range(n):
        values = slot_grad[place[k] * capacity : (place[k] + 1) * capacity].reshape(1, capacity)
        if k:
            values = lax.ppermute(values, "expert", [(j, (j - k) % n) for j in range(n)])
        expert = (me + k) % n
        got = contract_rows(selection(expert_ids, expert, capacity), values.reshape(capacity, 1))
        token_route = token_route + jnp.where(expert_ids == expert, got, 0.0)
    route_grad = token_route.astype(bf16)

    slot_normed = after(slot_normed, route_grad)
    slot_blocks = [
        slot_normed[place[k] * capacity : (place[k] + 1) * capacity] for k in range(n)
    ]
    grad_normed = line_backward(slot_blocks, mine, to_last, to_first, n)

    scaled_normed = grad_normed * norm_gain
    branch = inv_rms * (
        scaled_normed - unit_rows * jnp.mean(scaled_normed * unit_rows, axis=-1, keepdims=True)
    )
    grad_residual = (grad_out.astype(f32) + branch).astype(bf16)

    grad_in = jnp.zeros((), f32)
    grad_down = jnp.zeros((), f32)
    if groups == 8 and n_ul == 2:
        bundles = [[0, 2], [4, 6, 1, 3], [5, 7]]
    else:
        bundles = [[mask] for mask in range(groups)]

    def pick(cols, mask):
        return lax.dynamic_index_in_dim(cols, spot ^ mask, axis=0, keepdims=False)

    for bundle in bundles:
        inners = jnp.concatenate([inner_of[m] for m in bundle], axis=0)
        left_in = jnp.concatenate([pick(cols_normed, m) for m in bundle], axis=0)
        left_down = jnp.concatenate(
            [pick(cols, m) for m in bundle for cols in (cols_early, cols_late)], axis=0
        )
        grad_in = grad_in + contract_rows(left_in, inners[:, : 2 * hid])
        grad_down = grad_down + contract_rows(left_down, inners[:, 2 * hid :])
    return (grad_residual, route_grad, grad_in[None], grad_down[None])


def solution(mesh):
    rows = P(("dp", "ulysses", "expert"), None)
    return jax.shard_map(
        per_device,
        mesh=mesh,
        in_specs=(rows, P(), rows, rows, rows, P("expert", None, None), P("expert", None, None)),
        out_specs=(
            rows,
            rows,
            P("expert", ("dp", "ulysses"), None),
            P("expert", ("dp", "ulysses"), None),
        ),
        check_vma=False,
    )
```

```python
import jax
import jax.numpy as jnp
from jax import lax
from jax.sharding import PartitionSpec as P

eps = 1e-06
f32 = jnp.float32
bf16 = jnp.bfloat16


def dot(left, right):
    return jnp.dot(left, right, preferred_element_type=f32)


def contract_rows(left, right):
    return lax.dot_general(left, right, (((0,), (0,)), ((), ())), preferred_element_type=f32)


def contract_cols(left, right):
    return lax.dot_general(left, right, (((1,), (1,)), ((), ())), preferred_element_type=f32)


def after(value, *others):
    return lax.optimization_barrier((value, *others))[0]


def selection(ids, expert, capacity):
    tokens = ids.shape[0]
    hit = jnp.any(ids == expert, axis=1)
    row = lax.broadcasted_iota(jnp.int32, (tokens, tokens), 0)
    col = lax.broadcasted_iota(jnp.int32, (tokens, tokens), 1)
    rank = jnp.sum(jnp.where((row < col) & hit[:, None], 1, 0), axis=0)
    slots = lax.broadcasted_iota(jnp.int32, (capacity, tokens), 0)
    return ((slots == rank[None, :]) & hit[None, :]).astype(bf16)


def line_forward(rows, mine, to_last, to_first, n):
    raw = [None] * n
    packed = [[] for _ in range(n)]
    raw_parts = [[] for _ in range(n)]
    right, left = rows, rows
    for t in range(1, n):
        packed[t].append(
            lax.ppermute(dot(to_last[t - 1], right).astype(bf16), "expert", [(n - 2, n - 1)])
        )
        packed[n - t].append(
            lax.ppermute(dot(to_first[(n - t + 1) % n], left).astype(bf16), "expert", [(1, 0)])
        )
        pairs_right = [(j, j + 1) for j in range(t - 1, n - 2)]
        if pairs_right:
            right = lax.ppermute(right, "expert", pairs_right)
            left = lax.ppermute(left, "expert", [(n - 1 - a, n - 1 - b) for a, b in pairs_right])
            raw_parts[t].append(right)
            raw_parts[n - t].append(left)
    blocks = [dot(mine[0], rows).astype(bf16)]
    for k in range(1, n):
        block = None
        if raw_parts[k]:
            block = dot(mine[k], sum(raw_parts[k][1:], raw_parts[k][0])).astype(bf16)
        for part in packed[k]:
            block = part if block is None else block + part
        blocks.append(block)
    return blocks


def per_device(residual, norm_gain, grad_out, expert_ids, route_weights, weight_in, weight_down):
    tok_rows, width = residual.shape
    topk = expert_ids.shape[1]
    hid = weight_down.shape[1]
    n = lax.axis_size("expert")
    me = lax.axis_index("expert")
    capacity = min(tok_rows, 3 * tok_rows * topk // (2 * n))
    w_in, w_down = weight_in[0], weight_down[0]

    routes = jnp.concatenate([expert_ids.astype(f32), route_weights.astype(f32)], axis=1).T
    routes_of = [routes] + [
        lax.ppermute(routes, "expert", [(j, (j + k) % n) for j in range(n)]) for k in range(1, n)
    ]
    ids_of = [r[:topk].T.astype(jnp.int32) for r in routes_of]
    mine = [selection(ids, me, capacity) for ids in ids_of]
    to_last = [selection(ids, n - 1, capacity) for ids in ids_of]
    to_first = [selection(ids, 0, capacity) for ids in ids_of]
    weight_of = []
    for r, ids, m in zip(routes_of, ids_of, mine):
        w_tok = jnp.sum(jnp.where(ids == me, r[topk:].T, 0.0), axis=1, keepdims=True)
        weight_of.append(dot(m, w_tok.astype(bf16)))
    weight_col = jnp.concatenate(weight_of, axis=0)

    resid = residual.astype(f32)
    inv_rms = lax.rsqrt(jnp.mean(resid * resid, axis=-1, keepdims=True) + eps)
    unit_rows = resid * inv_rms
    normed = (unit_rows * norm_gain).astype(bf16)

    normed_rows = jnp.concatenate(line_forward(normed, mine, to_last, to_first, n), axis=0)
    grad_rows = jnp.concatenate(line_forward(grad_out, mine, to_last, to_first, n), axis=0)

    proj = dot(normed_rows, w_in)
    gate, up = proj[:, :hid], proj[:, hid:]
    sigmoid_gate = jax.nn.sigmoid(gate)
    silu_gate = gate * sigmoid_gate
    hidden = (silu_gate * up).astype(bf16)
    scaled = (weight_col * grad_rows.astype(f32)).astype(bf16)
    back = contract_cols(grad_rows, w_down)
    slot_grad = jnp.sum(back * hidden.astype(f32), axis=1).astype(bf16)
    grad_hidden = weight_col * back
    d_gate = grad_hidden * up * sigmoid_gate * (1.0 + gate * (1.0 - sigmoid_gate))
    d_up = grad_hidden * silu_gate
    d_proj = jnp.concatenate([d_gate, d_up], axis=1).astype(bf16)
    hidden, d_proj, scaled = lax.optimization_barrier((hidden, d_proj, scaled))

    spread = dict(scatter_dimension=0, tiled=True)
    part_down = contract_rows(scaled, hidden).astype(bf16)
    sum_down = lax.psum_scatter(part_down, ("dp", "ulysses"), **spread)
    part_in = contract_rows(normed_rows, d_proj).astype(bf16)
    sum_in = lax.psum_scatter(part_in, ("dp", "ulysses"), **spread)
    grad_in = sum_in.astype(f32)
    grad_down = sum_down.astype(f32)

    token_route = jnp.zeros((tok_rows, topk), f32)
    for k in range(n):
        values = slot_grad[k * capacity : (k + 1) * capacity].reshape(1, capacity)
        if k:
            values = lax.ppermute(values, "expert", [(j, (j - k) % n) for j in range(n)])
        expert = (me + k) % n
        got = contract_rows(selection(expert_ids, expert, capacity), values.reshape(capacity, 1))
        token_route = token_route + jnp.where(expert_ids == expert, got, 0.0)
    route_grad = token_route.astype(bf16)

    slot_normed = contract_cols(after(d_proj, part_in), w_in).astype(bf16)
    homes, slots = [], []
    for k in range(n):
        block = slot_normed[k * capacity : (k + 1) * capacity]
        if k:
            block = lax.ppermute(block, "expert", [(j, (j - k) % n) for j in range(n)])
        homes.append(selection(expert_ids, (me + k) % n, capacity))
        slots.append(block)
    grad_normed = contract_rows(jnp.concatenate(homes, axis=0), jnp.concatenate(slots, axis=0))

    scaled_normed = grad_normed * norm_gain
    branch = inv_rms * (
        scaled_normed - unit_rows * jnp.mean(scaled_normed * unit_rows, axis=-1, keepdims=True)
    )
    grad_residual = (grad_out.astype(f32) + branch).astype(bf16)

    return (grad_residual, route_grad, grad_in[None], grad_down[None])


def solution(mesh):
    rows = P(("dp", "ulysses", "expert"), None)
    return jax.shard_map(
        per_device,
        mesh=mesh,
        in_specs=(rows, P(), rows, rows, rows, P("expert", None, None), P("expert", None, None)),
        out_specs=(
            rows,
            rows,
            P("expert", ("dp", "ulysses"), None),
            P("expert", ("dp", "ulysses"), None),
        ),
        check_vma=False,
    )
```

```python
import jax
import jax.numpy as jnp
from jax import lax
from jax.sharding import PartitionSpec as P

eps = 1e-06
f32 = jnp.float32
bf16 = jnp.bfloat16


def dot(left, right):
    return jnp.dot(left, right, preferred_element_type=f32)


def contract_rows(left, right):
    return lax.dot_general(left, right, (((0,), (0,)), ((), ())), preferred_element_type=f32)


def contract_cols(left, right):
    return lax.dot_general(left, right, (((1,), (1,)), ((), ())), preferred_element_type=f32)


def after(value, *others):
    return lax.optimization_barrier((value, *others))[0]


def selection(ids, expert, capacity):
    tokens = ids.shape[0]
    hit = jnp.any(ids == expert, axis=1)
    row = lax.broadcasted_iota(jnp.int32, (tokens, tokens), 0)
    col = lax.broadcasted_iota(jnp.int32, (tokens, tokens), 1)
    rank = jnp.sum(jnp.where((row < col) & hit[:, None], 1, 0), axis=0)
    slots = lax.broadcasted_iota(jnp.int32, (capacity, tokens), 0)
    return ((slots == rank[None, :]) & hit[None, :]).astype(bf16)


def line_forward(rows, mine, to_last, to_first, n):
    raw = [None] * n
    packed = [[] for _ in range(n)]
    raw_parts = [[] for _ in range(n)]
    right, left = rows, rows
    for t in range(1, n):
        packed[t].append(
            lax.ppermute(dot(to_last[t - 1], right).astype(bf16), "expert", [(n - 2, n - 1)])
        )
        packed[n - t].append(
            lax.ppermute(dot(to_first[(n - t + 1) % n], left).astype(bf16), "expert", [(1, 0)])
        )
        pairs_right = [(j, j + 1) for j in range(t - 1, n - 2)]
        if pairs_right:
            right = lax.ppermute(right, "expert", pairs_right)
            left = lax.ppermute(left, "expert", [(n - 1 - a, n - 1 - b) for a, b in pairs_right])
            raw_parts[t].append(right)
            raw_parts[n - t].append(left)
    blocks = [dot(mine[0], rows).astype(bf16)]
    for k in range(1, n):
        block = None
        if raw_parts[k]:
            block = dot(mine[k], sum(raw_parts[k][1:], raw_parts[k][0])).astype(bf16)
        for part in packed[k]:
            block = part if block is None else block + part
        blocks.append(block)
    return blocks


def per_device(residual, norm_gain, grad_out, expert_ids, route_weights, weight_in, weight_down):
    tok_rows, width = residual.shape
    topk = expert_ids.shape[1]
    hid = weight_down.shape[1]
    n = lax.axis_size("expert")
    me = lax.axis_index("expert")
    capacity = min(tok_rows, 3 * tok_rows * topk // (2 * n))
    w_in, w_down = weight_in[0], weight_down[0]

    routes = jnp.concatenate([expert_ids.astype(f32), route_weights.astype(f32)], axis=1).T
    routes_of = [routes] + [
        lax.ppermute(routes, "expert", [(j, (j + k) % n) for j in range(n)]) for k in range(1, n)
    ]
    ids_of = [r[:topk].T.astype(jnp.int32) for r in routes_of]
    mine = [selection(ids, me, capacity) for ids in ids_of]
    to_last = [selection(ids, n - 1, capacity) for ids in ids_of]
    to_first = [selection(ids, 0, capacity) for ids in ids_of]
    weight_of = []
    for r, ids, m in zip(routes_of, ids_of, mine):
        w_tok = jnp.sum(jnp.where(ids == me, r[topk:].T, 0.0), axis=1, keepdims=True)
        weight_of.append(dot(m, w_tok.astype(bf16)))
    weight_col = jnp.concatenate(weight_of, axis=0)

    resid = residual.astype(f32)
    inv_rms = lax.rsqrt(jnp.mean(resid * resid, axis=-1, keepdims=True) + eps)
    unit_rows = resid * inv_rms
    normed = (unit_rows * norm_gain).astype(bf16)

    normed_rows = jnp.concatenate(line_forward(normed, mine, to_last, to_first, n), axis=0)
    grad_rows = jnp.concatenate(line_forward(grad_out, mine, to_last, to_first, n), axis=0)

    proj = dot(normed_rows, w_in)
    gate, up = proj[:, :hid], proj[:, hid:]
    sigmoid_gate = jax.nn.sigmoid(gate)
    silu_gate = gate * sigmoid_gate
    hidden = (silu_gate * up).astype(bf16)
    scaled = (weight_col * grad_rows.astype(f32)).astype(bf16)
    back = contract_cols(grad_rows, w_down)
    slot_grad = jnp.sum(back * hidden.astype(f32), axis=1).astype(bf16)
    grad_hidden = weight_col * back
    d_gate = grad_hidden * up * sigmoid_gate * (1.0 + gate * (1.0 - sigmoid_gate))
    d_up = grad_hidden * silu_gate
    d_proj = jnp.concatenate([d_gate, d_up], axis=1).astype(bf16)
    hidden, d_proj, scaled = lax.optimization_barrier((hidden, d_proj, scaled))

    partial = jnp.concatenate(
        [contract_rows(normed_rows, d_proj), contract_rows(scaled, hidden)], axis=1
    ).astype(bf16)
    summed = lax.psum_scatter(
        partial, ("dp", "ulysses"), scatter_dimension=0, tiled=True
    ).astype(f32)
    grad_in = summed[:, : 2 * hid]
    grad_down = summed[:, 2 * hid :]

    token_route = jnp.zeros((tok_rows, topk), f32)
    for k in range(n):
        values = slot_grad[k * capacity : (k + 1) * capacity].reshape(1, capacity)
        if k:
            values = lax.ppermute(values, "expert", [(j, (j - k) % n) for j in range(n)])
        expert = (me + k) % n
        got = contract_rows(selection(expert_ids, expert, capacity), values.reshape(capacity, 1))
        token_route = token_route + jnp.where(expert_ids == expert, got, 0.0)
    route_grad = token_route.astype(bf16)

    slot_normed = contract_cols(after(d_proj, partial), w_in).astype(bf16)
    homes, slots = [], []
    for k in range(n):
        block = slot_normed[k * capacity : (k + 1) * capacity]
        if k:
            block = lax.ppermute(block, "expert", [(j, (j - k) % n) for j in range(n)])
        homes.append(selection(expert_ids, (me + k) % n, capacity))
        slots.append(block)
    grad_normed = contract_rows(jnp.concatenate(homes, axis=0), jnp.concatenate(slots, axis=0))

    scaled_normed = grad_normed * norm_gain
    branch = inv_rms * (
        scaled_normed - unit_rows * jnp.mean(scaled_normed * unit_rows, axis=-1, keepdims=True)
    )
    grad_residual = (grad_out.astype(f32) + branch).astype(bf16)

    return (grad_residual, route_grad, grad_in[None], grad_down[None])


def solution(mesh):
    rows = P(("dp", "ulysses", "expert"), None)
    return jax.shard_map(
        per_device,
        mesh=mesh,
        in_specs=(rows, P(), rows, rows, rows, P("expert", None, None), P("expert", None, None)),
        out_specs=(
            rows,
            rows,
            P("expert", ("dp", "ulysses"), None),
            P("expert", ("dp", "ulysses"), None),
        ),
        check_vma=False,
    )
```
